512 devices in a mesh: shard: 16 (over x_lo, y, core), loop: 32 (over x_hi, z).
Axes of the slice: x: 4 (x_hi: 2, x_lo: 2; x = x_hi * 2 + x_lo), y: 4, z: 16, core: 2. Of those that a mesh axis runs over, the one named last changes fastest.
Arguments:
- hidden: bfloat16 [983040, 768], P(('shard', 'loop')), may hold values from -6 to 6
- segment: int32 [983040], P(('shard', 'loop')), may hold values from 0 to 8, as said below
- counts: int32 [4096], P(('shard', 'loop')), may hold values from 1 to 720, as said below
- w_proj: bfloat16 [768, 128], replicated, may hold values from -0.21875 to 0.21875
- seeds: bfloat16 [256, 32, 128], P('loop', 'shard'), may hold values from -6 to 6
Outputs:
- scores: float32 [4096, 256], P(('shard', 'loop'))
The draws below stay inside these ranges and needn't reach their ends.
Inputs may be any that keep to these rules, and one draw needn't show every extreme that they name: On every device one document has exactly 720 tokens, and a device's counts sum to less than 1920. `segment`: within a device, document k occupies counts of that document consecutive slots, documents in order of k from the first slot; all later slots hold 8, and every device has at least one such slot.
All inputs are finite; a program needn't handle non-finite values.
Results may differ from the reference program's by a relative error of at most 0.00055.
Values may be sent and summed in bfloat16 or wider, within the bound.
A program may use at most 64 MiB of HBM per device.

```python
import jax
import jax.numpy as jnp
from jax import lax

D_IN = 768
D = 128
QT = 32
Q = 256
MAXLEN = 720
DOC_DEV = 8
ROWS_DEV = 1920
DOCS = 4096
ROWS = 983040
N_LOOP = 32


def length_table(key):
    device_count = DOCS // DOC_DEV
    others = min(MAXLEN, (ROWS_DEV - MAXLEN - 1) // (DOC_DEV - 1))
    base = jax.random.randint(jax.random.fold_in(key, 11), (device_count, DOC_DEV), 1, others + 1)
    chosen = jax.random.randint(jax.random.fold_in(key, 12), (device_count,), 0, DOC_DEV)
    slots = jnp.arange(DOC_DEV, dtype=jnp.int32)[None, :]
    return jnp.where(slots == chosen[:, None], MAXLEN, base).astype(jnp.int32)


def draw_counts(key, part):
    return length_table(key).reshape(DOCS)


def draw_segment(key, part):
    table = length_table(key)
    ends = jnp.cumsum(table, axis=1)
    places = jnp.arange(ROWS_DEV, dtype=jnp.int32)
    labels = jnp.sum((places[None, :, None] >= ends[:, None, :]).astype(jnp.int32), axis=-1)
    return labels.reshape(ROWS).astype(jnp.int32)


def steps_of(own_key, dims, cuts, low, high):
    gain, own = 1.0, jax.random.fold_in(own_key, 6)
    for dim, parts in cuts:
        steps = jnp.exp(jax.random.uniform(jax.random.fold_in(own, dim), (parts,), jnp.float32, low / len(cuts), high / len(cuts)))
        gain = gain * jnp.repeat(steps, dims[dim] // parts).reshape([-1 if axis == dim else 1 for axis in range(len(dims))])
    return gain


def scatter_about(rng, extent, deviation, limit, cuts=(), kind=jnp.bfloat16):
    values = jax.random.normal(rng, extent, jnp.float32) * deviation
    if len(cuts) > 0:
        values = steps_of(rng, extent, cuts, -0.22, 0.18) * values
    return jnp.clip(values, min=-limit, max=limit).astype(kind)


def setup_inputs(seed: int = 0) -> dict:
    keys = jax.random.split(jax.random.key(seed), 6)
    hidden = scatter_about(keys[0], (ROWS, D_IN), 1.0, 6.0, ((0, 512),))
    segment = draw_segment(jax.random.fold_in(keys[5], 71), 0)
    counts = draw_counts(jax.random.fold_in(keys[5], 71), 0)
    w_proj = scatter_about(keys[3], (D_IN, D), D_IN ** -0.5, 0.21875)
    seeds = scatter_about(keys[4], (Q, QT, D), 1.0, 6.0, ((0, 32), (1, 16)))
    return {"hidden": hidden, "segment": segment, "counts": counts, "w_proj": w_proj, "seeds": seeds}


BETA = 16.0
EPS = 1e-06

def unit_rows(values):
    values = values.astype(jnp.float32)
    return (values * lax.rsqrt(lax.optimization_barrier(jnp.sum(values * values, axis=-1, keepdims=True)) + EPS)).astype(jnp.bfloat16)

def reference(hidden, segment, counts, w_proj, seeds):
    projected = jnp.dot(hidden, w_proj, preferred_element_type=jnp.float32)
    doc_vectors = unit_rows(projected)
    seed_vectors = unit_rows(seeds)
    device_count = DOCS // DOC_DEV
    group = Q // N_LOOP
    blocks = seed_vectors.reshape(N_LOOP, group * QT, D)
    vectors = doc_vectors.reshape(device_count, ROWS_DEV, D)
    labels = segment.reshape(device_count, ROWS_DEV).astype(jnp.int32)
    sizes = counts.reshape(device_count, DOC_DEV).astype(jnp.float32)

    def one_device(item):
        rows, ids, lengths = item

        def one_block(block):
            sims = jnp.dot(rows, block.T, preferred_element_type=jnp.float32)
            mass = jax.ops.segment_sum(jnp.exp(BETA * sims), ids, num_segments=DOC_DEV + 1)[:DOC_DEV]
            logs = jnp.log(mass / lengths[:, None]).reshape(DOC_DEV, group, QT)
            return lax.optimization_barrier(jnp.mean(logs, axis=-1))
        result = lax.map(one_block, blocks)
        return jnp.transpose(result, (1, 0, 2)).reshape(DOC_DEV, Q)
    result = lax.map(one_device, (vectors, labels, sizes))
    return result.reshape(DOCS, Q)
```

```python
import math

import jax
import jax.numpy as jnp
from jax import lax
from jax.experimental import pallas as pl
from jax.experimental.pallas import tpu as pltpu
from jax.sharding import PartitionSpec as P

BETA = 16.0
EPS = 1e-06
NX, NY, NZ = 4, 4, 16
ROWS, D_IN, D = 1920, 768, 128
SHARDS, LOOPS = 16, 32
MESH = pl.DeviceIdType.MESH
VMEM_LIMIT = 60 * 1024 * 1024


def unit_rows(values):
    values = values.astype(jnp.float32)
    return (values * lax.rsqrt(jnp.sum(values * values, axis=-1, keepdims=True) + EPS)).astype(
        jnp.bfloat16
    )


def gather_steps(own, buf, local_sem, send_z, recv_z, send_h, recv_h, send_c, recv_c):
    me_s = lax.axis_index("shard")
    me_l = lax.axis_index("loop")
    core, y, x_lo = me_s % 2, (me_s // 2) % NY, me_s // (2 * NY)
    x_hi, z = me_l // NZ, me_l % NZ
    x = 2 * x_hi + x_lo

    def device(px, py, pz, pc):
        return (((px % 2) * NY + py) * 2 + pc, (px // 2) * NZ + pz)

    def moved(value, by, size):
        return (value + by + size) % size

    def place(half, a, b, c, low=0, count=8):
        dx, dy = (a, b) if half == 0 else (b, a)
        px, py = moved(x, dx, NX), moved(y, dy, NY)
        return buf.at[((px % 2) * NY + py) * 2 + c, pl.ds((px // 2) * NZ + 8 * half + low, count)]

    def neighbour(half, order, by):
        if (half == 0) == (order == 0):
            return device(moved(x, by, NX), y, z, core)
        return device(x, moved(y, by, NY), z, core)

    barrier = pltpu.get_barrier_semaphore()
    partners = [device(x, y, moved(z, k, NZ), core) for k in range(1, NZ)]
    partners += [neighbour(0, 0, 1), neighbour(0, 0, -1), neighbour(0, 1, 1), neighbour(0, 1, -1)]
    partners += [device(x, y, z, 1 - core)]
    for partner in partners:
        pl.semaphore_signal(barrier, inc=1, device_id=partner, device_id_type=MESH)
    pl.semaphore_wait(barrier, len(partners))

    sent = []

    def remote(src, dst, send, recv, target):
        return pltpu.make_async_remote_copy(
            src_ref=src, dst_ref=dst, send_sem=send, recv_sem=recv, device_id=target, device_id_type=MESH
        )

    def z_copy(k, block):
        return remote(own, block, send_z.at[k], recv_z.at[k], device(x, y, moved(z, k, NZ), core))

    def start(copy):
        copy.start()
        sent.append(copy)

    mine = pltpu.make_async_copy(own, buf.at[me_s, me_l], local_sem)
    mine.start()
    for k in (8, 7, 9, 6, 10, 5, 11, 4, 12, 3, 13, 2, 14, 1, 15):
        start(z_copy(k, buf.at[me_s, me_l]))
    mine.wait()
    for k in range(1, NZ):
        z_copy(k, buf.at[me_s, x_hi * NZ + moved(z, -k, NZ)]).wait_recv()

    def hop(half, index, kind, ref, order):
        by = 1 if kind in (0, 2) else -1
        return remote(
            ref, ref, send_h.at[half, index, kind], recv_h.at[half, index, kind], neighbour(half, order, by)
        )

    def cross(half, a, b, c):
        ref = place(half, a, b, c)
        slot = (half * 4 + a % 4) * 4 + b % 4
        return remote(ref, ref, send_c.at[slot], recv_c.at[slot], device(x, y, z, 1 - core))

    def ready_first(half, a):
        start(hop(half, a % 4, 0, place(half, a, 0, core), 1))
        start(hop(half, a % 4, 1, place(half, a, 0, core), 1))
        start(cross(half, a, 0, core))

    halves = (0, 1)
    for half in halves:
        own_slab = place(half, 0, 0, core)
        start(hop(half, 4, 0, own_slab, 0))
        start(hop(half, 4, 1, own_slab, 0))
    for half in halves:
        ready_first(half, 0)
    for half in halves:
        hop(half, 4, 0, place(half, -1, 0, core), 0).wait_recv()
        start(hop(half, 4, 2, place(half, -1, 0, core, 0, 4), 0))
        hop(half, 4, 1, place(half, 1, 0, core), 0).wait_recv()
        start(hop(half, 4, 3, place(half, 1, 0, core, 4, 4), 0))
    for half in halves:
        ready_first(half, -1)
        ready_first(half, 1)

    def wait_second(half, a):
        hop(half, a % 4, 0, place(half, a, -1, core), 1).wait_recv()
        start(hop(half, a % 4, 2, place(half, a, -1, core, 0, 4), 1))
        hop(half, a % 4, 1, place(half, a, 1, core), 1).wait_recv()
        start(hop(half, a % 4, 3, place(half, a, 1, core, 4, 4), 1))
        start(cross(half, a, -1, core))
        start(cross(half, a, 1, core))

    for half in halves:
        hop(half, 4, 2, place(half, 2, 0, core, 0, 4), 0).wait_recv()
        hop(half, 4, 3, place(half, 2, 0, core, 4, 4), 0).wait_recv()
        ready_first(half, 2)
    for a in (0, -1, 1, 2):
        for half in halves:
            wait_second(half, a)
    for a in (0, -1, 1, 2):
        for half in halves:
            hop(half, a % 4, 2, place(half, a, 2, core, 0, 4), 1).wait_recv()
            hop(half, a % 4, 3, place(half, a, 2, core, 4, 4), 1).wait_recv()
            start(cross(half, a, 2, core))
    for b in (0, -1, 1, 2):
        for a in (0, -1, 1, 2):
            for half in halves:
                cross(half, a, b, 1 - core).wait_recv()
    for copy in sent:
        copy.wait_send()


def gather_kernel(own, out, buf, local_sem, send_z, recv_z, send_h, recv_h, send_c, recv_c):
    gather_steps(own, buf, local_sem, send_z, recv_z, send_h, recv_h, send_c, recv_c)
    final = pltpu.make_async_copy(buf, out, local_sem)
    final.start()
    final.wait()


def gather_blocks(block):
    dma = pltpu.SemaphoreType.DMA
    shape = (SHARDS, LOOPS) + block.shape
    return pl.pallas_call(
        gather_kernel,
        out_shape=jax.ShapeDtypeStruct(shape, block.dtype),
        in_specs=[pl.BlockSpec(memory_space=pltpu.VMEM)],
        out_specs=pl.BlockSpec(memory_space=pl.ANY),
        scratch_shapes=[
            pltpu.VMEM(shape, block.dtype),
            dma,
            dma((NZ,)),
            dma((NZ,)),
            dma((2, 5, 4)),
            dma((2, 5, 4)),
            dma((32,)),
            dma((32,)),
        ],
        compiler_params=pltpu.CompilerParams(collective_id=0, has_side_effects=True),
        name="seed_gather",
    )(block)


COLS = 512
CHUNKS = [(start, min(256, ROWS - start)) for start in range(0, ROWS, 256)]


def score_kernel(hidden, segment, counts, w_proj, seeds, out, vectors, member):
    for start in range(0, ROWS, 384):
        projected = jnp.dot(
            hidden[pl.ds(start, 384), :], w_proj[...], preferred_element_type=jnp.float32
        )
        vectors[pl.ds(start, 384), :] = unit_rows(projected)
    docs = lax.broadcasted_iota(jnp.int32, (16, ROWS), 0)
    member[...] = jnp.where(segment[...] == docs, 1.0, 0.0).astype(jnp.bfloat16)
    lengths = counts[...].astype(jnp.float32)

    def step(index, total):
        block = seeds[pl.ds(pl.multiple_of(index * COLS, COLS), COLS), :]
        mass = jnp.zeros((16, COLS), jnp.float32)
        for start, size in CHUNKS:
            sims = lax.dot_general(
                vectors[pl.ds(start, size), :],
                block,
                (((1,), (1,)), ((), ())),
                preferred_element_type=jnp.float32,
            )
            weights = jnp.exp2(sims * (BETA * math.log2(math.e))).astype(jnp.bfloat16)
            mass = mass + jnp.dot(
                member[:, pl.ds(start, size)], weights, preferred_element_type=jnp.float32
            )
        return total + jnp.log(mass[:8] / lengths)

    total = lax.fori_loop(0, SHARDS, step, jnp.zeros((8, COLS), jnp.float32))
    pairs = (
        lax.broadcasted_iota(jnp.int32, (COLS, COLS // 2), 0) // 2
        == lax.broadcasted_iota(jnp.int32, (COLS, COLS // 2), 1)
    ).astype(jnp.float32)
    out[...] = jnp.dot(
        total * (1.0 / 32.0), pairs, precision=lax.Precision.HIGHEST, preferred_element_type=jnp.float32
    )


def body(hidden, segment, counts, w_proj, seeds):
    block = unit_rows(seeds).reshape(16, D)
    gathered = gather_blocks(block).reshape(SHARDS * LOOPS * 16, D)
    return pl.pallas_call(
        score_kernel,
        out_shape=jax.ShapeDtypeStruct((8, 256), jnp.float32),
        scratch_shapes=[pltpu.VMEM((ROWS, D), jnp.bfloat16), pltpu.VMEM((16, ROWS), jnp.bfloat16)],
        compiler_params=pltpu.CompilerParams(vmem_limit_bytes=VMEM_LIMIT),
        name="soft_maxsim",
    )(hidden, segment.reshape(1, ROWS), counts.reshape(8, 1), w_proj, gathered)


def solution(mesh):
    in_specs = (
        P(("shard", "loop"), None),
        P(("shard", "loop")),
        P(("shard", "loop")),
        P(),
        P("loop", "shard", None),
    )
    out_specs = P(("shard", "loop"), None)
    return jax.shard_map(body, mesh=mesh, in_specs=in_specs, out_specs=out_specs, check_vma=False)
```

```python
import math

import jax
import jax.numpy as jnp
from jax import lax
from jax.experimental import pallas as pl
from jax.experimental.pallas import tpu as pltpu
from jax.sharding import PartitionSpec as P

BETA = 16.0
EPS = 1e-06
NX, NY, NZ = 4, 4, 16
ROWS, D_IN, D = 1920, 768, 128
SHARDS, LOOPS = 16, 32
MESH = pl.DeviceIdType.MESH
VMEM_LIMIT = 60 * 1024 * 1024


def unit_rows(values):
    values = values.astype(jnp.float32)
    return (values * lax.rsqrt(jnp.sum(values * values, axis=-1, keepdims=True) + EPS)).astype(
        jnp.bfloat16
    )


def gather_steps(own, buf, local_sem, send_z, recv_z, send_h, recv_h, send_c, recv_c):
    me_s = lax.axis_index("shard")
    me_l = lax.axis_index("loop")
    core, y, x_lo = me_s % 2, (me_s // 2) % NY, me_s // (2 * NY)
    x_hi, z = me_l // NZ, me_l % NZ
    x = 2 * x_hi + x_lo

    def device(px, py, pz, pc):
        return (((px % 2) * NY + py) * 2 + pc, (px // 2) * NZ + pz)

    def moved(value, by, size):
        return (value + by + size) % size

    def place(half, a, b, c, low=0, count=8):
        dx, dy = (a, b) if half == 0 else (b, a)
        px, py = moved(x, dx, NX), moved(y, dy, NY)
        return buf.at[((px % 2) * NY + py) * 2 + c, pl.ds((px // 2) * NZ + 8 * half + low, count)]

    def neighbour(half, order, by):
        if (half == 0) == (order == 0):
            return device(moved(x, by, NX), y, z, core)
        return device(x, moved(y, by, NY), z, core)

    barrier = pltpu.get_barrier_semaphore()
    partners = [device(x, y, moved(z, k, NZ), core) for k in range(1, NZ)]
    partners += [neighbour(0, 0, 1), neighbour(0, 0, -1), neighbour(0, 1, 1), neighbour(0, 1, -1)]
    partners += [device(x, y, z, 1 - core)]
    for partner in partners:
        pl.semaphore_signal(barrier, inc=1, device_id=partner, device_id_type=MESH)
    pl.semaphore_wait(barrier, len(partners))

    sent = []

    def remote(src, dst, send, recv, target):
        return pltpu.make_async_remote_copy(
            src_ref=src, dst_ref=dst, send_sem=send, recv_sem=recv, device_id=target, device_id_type=MESH
        )

    def z_copy(k, block):
        return remote(own, block, send_z.at[k], recv_z.at[k], device(x, y, moved(z, k, NZ), core))

    def start(copy):
        copy.start()
        sent.append(copy)

    mine = pltpu.make_async_copy(own, buf.at[me_s, me_l], local_sem)
    mine.start()
    for k in (8, 7, 9, 6, 10, 5, 11, 4, 12, 3, 13, 2, 14, 1, 15):
        start(z_copy(k, buf.at[me_s, me_l]))
    mine.wait()
    for k in range(1, NZ):
        z_copy(k, buf.at[me_s, x_hi * NZ + moved(z, -k, NZ)]).wait_recv()

    def hop(half, index, kind, ref, order):
        by = 1 if kind in (0, 2) else -1
        return remote(
            ref, ref, send_h.at[half, index, kind], recv_h.at[half, index, kind], neighbour(half, order, by)
        )

    def cross(half, a, b, c):
        ref = place(half, a, b, c)
        slot = (half * 4 + a % 4) * 4 + b % 4
        return remote(ref, ref, send_c.at[slot], recv_c.at[slot], device(x, y, z, 1 - core))

    def ready_first(half, a):
        start(hop(half, a % 4, 0, place(half, a, 0, core), 1))
        start(hop(half, a % 4, 1, place(half, a, 0, core), 1))
        start(cross(half, a, 0, core))

    halves = (0, 1)
    for half in halves:
        own_slab = place(half, 0, 0, core)
        start(hop(half, 4, 0, own_slab, 0))
        start(hop(half, 4, 1, own_slab, 0))
    for half in halves:
        ready_first(half, 0)
    for half in halves:
        hop(half, 4, 0, place(half, -1, 0, core), 0).wait_recv()
        start(hop(half, 4, 2, place(half, -1, 0, core, 0, 4), 0))
        hop(half, 4, 1, place(half, 1, 0, core), 0).wait_recv()
        start(hop(half, 4, 3, place(half, 1, 0, core, 4, 4), 0))
    for half in halves:
        ready_first(half, -1)
        ready_first(half, 1)

    def wait_second(half, a):
        hop(half, a % 4, 0, place(half, a, -1, core), 1).wait_recv()
        start(hop(half, a % 4, 2, place(half, a, -1, core, 0, 4), 1))
        hop(half, a % 4, 1, place(half, a, 1, core), 1).wait_recv()
        start(hop(half, a % 4, 3, place(half, a, 1, core, 4, 4), 1))
        start(cross(half, a, -1, core))
        start(cross(half, a, 1, core))

    for half in halves:
        hop(half, 4, 2, place(half, 2, 0, core, 0, 4), 0).wait_recv()
        hop(half, 4, 3, place(half, 2, 0, core, 4, 4), 0).wait_recv()
        ready_first(half, 2)
    for a in (0, -1, 1, 2):
        for half in halves:
            wait_second(half, a)
    for a in (0, -1, 1, 2):
        for half in halves:
            hop(half, a % 4, 2, place(half, a, 2, core, 0, 4), 1).wait_recv()
            hop(half, a % 4, 3, place(half, a, 2, core, 4, 4), 1).wait_recv()
            start(cross(half, a, 2, core))
    for b in (0, -1, 1, 2):
        for a in (0, -1, 1, 2):
            for half in halves:
                cross(half, a, b, 1 - core).wait_recv()
    for copy in sent:
        copy.wait_send()


def gather_kernel(own, out, buf, local_sem, send_z, recv_z, send_h, recv_h, send_c, recv_c):
    gather_steps(own, buf, local_sem, send_z, recv_z, send_h, recv_h, send_c, recv_c)
    final = pltpu.make_async_copy(buf, out, local_sem)
    final.start()
    final.wait()


def gather_blocks(block):
    dma = pltpu.SemaphoreType.DMA
    shape = (SHARDS, LOOPS) + block.shape
    return pl.pallas_call(
        gather_kernel,
        out_shape=jax.ShapeDtypeStruct(shape, block.dtype),
        in_specs=[pl.BlockSpec(memory_space=pltpu.VMEM)],
        out_specs=pl.BlockSpec(memory_space=pl.ANY),
        scratch_shapes=[
            pltpu.VMEM(shape, block.dtype),
            dma,
            dma((NZ,)),
            dma((NZ,)),
            dma((2, 5, 4)),
            dma((2, 5, 4)),
            dma((32,)),
            dma((32,)),
        ],
        compiler_params=pltpu.CompilerParams(collective_id=0, has_side_effects=True),
        name="seed_gather",
    )(block)


COLS = 512
LANES = 512
PIECES = LANES // COLS
CHUNKS = [(start, min(256, ROWS - start)) for start in range(0, ROWS, 256)]


def similarity(vectors, block, start, size):
    return lax.dot_general(
        vectors[pl.ds(start, size), :],
        block,
        (((1,), (1,)), ((), ())),
        preferred_element_type=jnp.float32,
    )


def overlapped(vectors, member, block, fill, drain):
    mass = jnp.zeros((16, COLS), jnp.float32)
    ahead = None
    if fill is not None:
        ahead = similarity(vectors, block, *CHUNKS[0])
    for position, (start, size) in enumerate(CHUNKS):
        now = ahead
        if fill is not None and position + 1 < len(CHUNKS):
            ahead = similarity(vectors, block, *CHUNKS[position + 1])
        if drain is not None:
            mass = mass + jnp.dot(
                member[:, pl.ds(start, size)],
                drain[pl.ds(start, size), :],
                preferred_element_type=jnp.float32,
            )
        if fill is not None:
            fill[pl.ds(start, size), :] = jnp.exp2(now * (BETA * math.log2(math.e))).astype(jnp.bfloat16)
    return mass[:8]


def score_kernel(hidden, counts, w_proj, seeds, out, vectors, member, totals, even, odd):
    for start in range(0, ROWS, 384):
        projected = jnp.dot(
            hidden[pl.ds(start, 384), :], w_proj[...], preferred_element_type=jnp.float32
        )
        vectors[pl.ds(start, 384), :] = unit_rows(projected)
    docs = lax.broadcasted_iota(jnp.int32, (16, ROWS), 0)
    slots = lax.broadcasted_iota(jnp.int32, (16, ROWS), 1)
    rows = lax.broadcasted_iota(jnp.int32, (8, COLS), 0)
    inside = jnp.zeros((16, ROWS), jnp.bool_)
    lengths = jnp.ones((8, COLS), jnp.float32)
    first = jnp.int32(0)
    for doc in range(8):
        last = first + counts[doc]
        inside = inside | ((docs == doc) & (slots >= first) & (slots < last))
        lengths = jnp.where(rows == doc, counts[doc].astype(jnp.float32), lengths)
        first = last
    member[...] = jnp.where(inside, 1.0, 0.0).astype(jnp.bfloat16)
    totals[...] = jnp.zeros_like(totals)

    def block_of(index):
        return seeds[pl.ds(pl.multiple_of(index * COLS, COLS), COLS), :]

    def add(index, mass):
        totals[index % PIECES] += jnp.log(mass / lengths)

    last = SHARDS * PIECES - 1
    overlapped(vectors, member, block_of(0), even, None)

    def step(pair, carry):
        add(2 * pair, overlapped(vectors, member, block_of(2 * pair + 1), odd, even))
        add(2 * pair + 1, overlapped(vectors, member, block_of(2 * pair + 2), even, odd))
        return carry

    lax.fori_loop(0, last // 2, step, 0)
    add(last - 1, overlapped(vectors, member, block_of(last), odd, even))
    add(last, overlapped(vectors, member, None, None, odd))
    pairs = (
        lax.broadcasted_iota(jnp.int32, (COLS, COLS // 2), 0) // 2
        == lax.broadcasted_iota(jnp.int32, (COLS, COLS // 2), 1)
    ).astype(jnp.float32)
    for piece in range(PIECES):
        out[:, pl.ds(piece * (COLS // 2), COLS // 2)] = jnp.dot(
            totals[piece] * (1.0 / 32.0),
            pairs,
            precision=lax.Precision.HIGHEST,
            preferred_element_type=jnp.float32,
        )


def body(hidden, segment, counts, w_proj, seeds):
    block = unit_rows(seeds).reshape(16, D)
    gathered = gather_blocks(block).reshape(SHARDS * LOOPS * 16, D)
    vmem = pl.BlockSpec(memory_space=pltpu.VMEM)
    return pl.pallas_call(
        score_kernel,
        out_shape=jax.ShapeDtypeStruct((8, 256), jnp.float32),
        in_specs=[vmem, pl.BlockSpec(memory_space=pltpu.SMEM), vmem, vmem],
        out_specs=vmem,
        scratch_shapes=[
            pltpu.VMEM((ROWS, D), jnp.bfloat16),
            pltpu.VMEM((16, ROWS), jnp.bfloat16),
            pltpu.VMEM((PIECES, 8, COLS), jnp.float32),
            pltpu.VMEM((ROWS, COLS), jnp.bfloat16),
            pltpu.VMEM((ROWS, COLS), jnp.bfloat16),
        ],
        compiler_params=pltpu.CompilerParams(vmem_limit_bytes=VMEM_LIMIT),
        name="soft_maxsim",
    )(hidden, counts, w_proj, gathered)


def solution(mesh):
    in_specs = (
        P(("shard", "loop"), None),
        P(("shard", "loop")),
        P(("shard", "loop")),
        P(),
        P("loop", "shard", None),
    )
    out_specs = P(("shard", "loop"), None)
    return jax.shard_map(body, mesh=mesh, in_specs=in_specs, out_specs=out_specs, check_vma=False)
```

```python
import math

import jax
import jax.numpy as jnp
from jax import lax
from jax.experimental import pallas as pl
from jax.experimental.pallas import tpu as pltpu
from jax.sharding import PartitionSpec as P

BETA = 16.0
EPS = 1e-06
NX, NY, NZ = 4, 4, 16
ROWS, D_IN, D = 1920, 768, 128
SHARDS, LOOPS = 16, 32
MESH = pl.DeviceIdType.MESH
VMEM_LIMIT = 60 * 1024 * 1024


def unit_rows(values):
    values = values.astype(jnp.float32)
    return (values * lax.rsqrt(jnp.sum(values * values, axis=-1, keepdims=True) + EPS)).astype(
        jnp.bfloat16
    )


COLS = 512
CHUNKS = [(start, min(256, ROWS - start)) for start in range(0, ROWS, 256)]


def similarity(vectors, block, start, size):
    return lax.dot_general(
        vectors[pl.ds(start, size), :],
        block,
        (((1,), (1,)), ((), ())),
        preferred_element_type=jnp.float32,
    )


def overlapped(vectors, member, block, fill, drain):
    mass = jnp.zeros((16, COLS), jnp.float32)
    ahead = None
    if fill is not None:
        ahead = similarity(vectors, block, *CHUNKS[0])
    for position, (start, size) in enumerate(CHUNKS):
        now = ahead
        if fill is not None and position + 1 < len(CHUNKS):
            ahead = similarity(vectors, block, *CHUNKS[position + 1])
        if drain is not None:
            mass = mass + jnp.dot(
                member[:, pl.ds(start, size)],
                drain[pl.ds(start, size), :],
                preferred_element_type=jnp.float32,
            )
        if fill is not None:
            fill[pl.ds(start, size), :] = jnp.exp2(now * (BETA * math.log2(math.e))).astype(jnp.bfloat16)
    return mass[:8]


def prepare(hidden, counts, w_proj, vectors, member, totals):
    for start in range(0, ROWS, 384):
        projected = jnp.dot(
            hidden[pl.ds(start, 384), :], w_proj[...], preferred_element_type=jnp.float32
        )
        vectors[pl.ds(start, 384), :] = unit_rows(projected)
    docs = lax.broadcasted_iota(jnp.int32, (16, ROWS), 0)
    slots = lax.broadcasted_iota(jnp.int32, (16, ROWS), 1)
    rows = lax.broadcasted_iota(jnp.int32, (8, COLS), 0)
    inside = jnp.zeros((16, ROWS), jnp.bool_)
    lengths = jnp.ones((8, COLS), jnp.float32)
    first = jnp.int32(0)
    for doc in range(8):
        last = first + counts[doc]
        inside = inside | ((docs == doc) & (slots >= first) & (slots < last))
        lengths = jnp.where(rows == doc, counts[doc].astype(jnp.float32), lengths)
        first = last
    member[...] = jnp.where(inside, 1.0, 0.0).astype(jnp.bfloat16)
    totals[...] = jnp.zeros_like(totals)
    return lengths


def fused_kernel(
    own, hidden, counts, w_proj, out,
    buf, rows_in, vectors, member, totals, even, odd,
    local_sem, hidden_sem, send_z, recv_z, send_h, recv_h, send_c, recv_c,
):
    fetch = pltpu.make_async_copy(hidden, rows_in, hidden_sem)
    fetch.start()
    me_s = lax.axis_index("shard")
    me_l = lax.axis_index("loop")
    core, y, x_lo = me_s % 2, (me_s // 2) % NY, me_s // (2 * NY)
    x_hi, z = me_l // NZ, me_l % NZ
    x = 2 * x_hi + x_lo

    def device(px, py, pz, pc):
        return (((px % 2) * NY + py) * 2 + pc, (px // 2) * NZ + pz)

    def moved(value, by, size):
        return (value + by + size) % size

    def place(half, a, b, c, low=0, count=8):
        dx, dy = (a, b) if half == 0 else (b, a)
        px, py = moved(x, dx, NX), moved(y, dy, NY)
        return buf.at[((px % 2) * NY + py) * 2 + c, pl.ds((px // 2) * NZ + 8 * half + low, count)]

    def neighbour(half, order, by):
        if (half == 0) == (order == 0):
            return device(moved(x, by, NX), y, z, core)
        return device(x, moved(y, by, NY), z, core)

    barrier = pltpu.get_barrier_semaphore()
    partners = [device(x, y, moved(z, k, NZ), core) for k in range(1, NZ)]
    partners += [neighbour(0, 0, 1), neighbour(0, 0, -1), neighbour(0, 1, 1), neighbour(0, 1, -1)]
    partners += [device(x, y, z, 1 - core)]
    for partner in partners:
        pl.semaphore_signal(barrier, inc=1, device_id=partner, device_id_type=MESH)
    pl.semaphore_wait(barrier, len(partners))

    sent = []

    def remote(src, dst, send, recv, target):
        return pltpu.make_async_remote_copy(
            src_ref=src, dst_ref=dst, send_sem=send, recv_sem=recv, device_id=target, device_id_type=MESH
        )

    def z_copy(k, block):
        return remote(own, block, send_z.at[k], recv_z.at[k], device(x, y, moved(z, k, NZ), core))

    def start(copy):
        copy.start()
        sent.append(copy)

    mine = pltpu.make_async_copy(own, buf.at[me_s, me_l], local_sem)
    mine.start()
    for k in (8, 7, 9, 6, 10, 5, 11, 4, 12, 3, 13, 2, 14, 1, 15):
        start(z_copy(k, buf.at[me_s, me_l]))
    fetch.wait()
    lengths = prepare(rows_in, counts, w_proj, vectors, member, totals)
    mine.wait()
    for k in range(1, NZ):
        z_copy(k, buf.at[me_s, x_hi * NZ + moved(z, -k, NZ)]).wait_recv()

    def hop(half, index, kind, ref, order):
        by = 1 if kind in (0, 2) else -1
        return remote(
            ref, ref, send_h.at[half, index, kind], recv_h.at[half, index, kind], neighbour(half, order, by)
        )

    def cross(half, a, b, c):
        ref = place(half, a, b, c)
        slot = (half * 4 + a % 4) * 4 + b % 4
        return remote(ref, ref, send_c.at[slot], recv_c.at[slot], device(x, y, z, 1 - core))

    def ready_first(half, a):
        start(hop(half, a % 4, 0, place(half, a, 0, core), 1))
        start(hop(half, a % 4, 1, place(half, a, 0, core), 1))
        start(cross(half, a, 0, core))

    halves = (0, 1)
    slabs = [(half, side) for half in halves for side in (-1, 1)]

    def first_arrived(half):
        hop(half, 4, 0, place(half, -1, 0, core), 0).wait_recv()
        start(hop(half, 4, 2, place(half, -1, 0, core, 0, 4), 0))
        hop(half, 4, 1, place(half, 1, 0, core), 0).wait_recv()
        start(hop(half, 4, 3, place(half, 1, 0, core, 4, 4), 0))
        ready_first(half, -1)
        ready_first(half, 1)

    def first_opposite(half):
        hop(half, 4, 2, place(half, 2, 0, core, 0, 4), 0).wait_recv()
        hop(half, 4, 3, place(half, 2, 0, core, 4, 4), 0).wait_recv()
        ready_first(half, 2)

    def second_arrived(half, a):
        hop(half, a % 4, 0, place(half, a, -1, core), 1).wait_recv()
        start(hop(half, a % 4, 2, place(half, a, -1, core, 0, 4), 1))
        hop(half, a % 4, 1, place(half, a, 1, core), 1).wait_recv()
        start(hop(half, a % 4, 3, place(half, a, 1, core, 4, 4), 1))
        start(cross(half, a, -1, core))
        start(cross(half, a, 1, core))

    def second_opposite(half, a):
        hop(half, a % 4, 2, place(half, a, 2, core, 0, 4), 1).wait_recv()
        hop(half, a % 4, 3, place(half, a, 2, core, 4, 4), 1).wait_recv()
        start(cross(half, a, 2, core))

    scratch = (even, odd)
    done = []

    def drained(block, fill, drain):
        mass = overlapped(vectors, member, block, fill, drain)
        if drain is not None:
            totals[done[-1]] += jnp.log(mass / lengths)

    def score(dx, dy):
        cross(0, dx, dy, 1 - core).wait_recv()
        cross(1, dy, dx, 1 - core).wait_recv()
        px, py = moved(x, dx, NX), moved(y, dy, NY)
        block = buf[pl.ds(((px % 2) * NY + py) * 2, 2), pl.ds((px // 2) * NZ, NZ)].reshape(COLS, D)
        turn = len(done)
        drained(block, scratch[turn % 2], scratch[(turn - 1) % 2] if turn else None)
        done.append(px // 2)

    for half in halves:
        own_slab = place(half, 0, 0, core)
        start(hop(half, 4, 0, own_slab, 0))
        start(hop(half, 4, 1, own_slab, 0))
    for half in halves:
        ready_first(half, 0)
    score(0, 0)
    for half in halves:
        first_arrived(half)
    for half in halves:
        second_arrived(half, 0)
    score(1, 0)
    for half in halves:
        first_opposite(half)
    score(-1, 0)
    for half in halves:
        second_opposite(half, 0)
    score(0, 1)
    for half, side in slabs:
        second_arrived(half, side)
    score(0, -1)
    for half in halves:
        second_arrived(half, 2)
    score(2, 0)
    for half, side in slabs:
        second_opposite(half, side)
    score(0, 2)
    for half in halves:
        second_opposite(half, 2)
    for dx, dy in ((1, 1), (1, -1), (-1, 1), (-1, -1), (2, 1), (2, -1), (1, 2), (-1, 2), (2, 2)):
        score(dx, dy)
    drained(None, None, scratch[(len(done) - 1) % 2])
    pairs = (
        lax.broadcasted_iota(jnp.int32, (COLS // 2, COLS // 4), 0) // 2
        == lax.broadcasted_iota(jnp.int32, (COLS // 2, COLS // 4), 1)
    ).astype(jnp.float32)
    for side in range(2):
        both = totals[side][:, : COLS // 2] + totals[side][:, COLS // 2 :]
        out[:, pl.ds(side * (COLS // 4), COLS // 4)] = jnp.dot(
            both * (1.0 / 32.0),
            pairs,
            precision=lax.Precision.HIGHEST,
            preferred_element_type=jnp.float32,
        )
    for copy in sent:
        copy.wait_send()


def body(hidden, segment, counts, w_proj, seeds):
    block = unit_rows(seeds).reshape(16, D)
    vmem = pl.BlockSpec(memory_space=pltpu.VMEM)
    dma = pltpu.SemaphoreType.DMA
    return pl.pallas_call(
        fused_kernel,
        out_shape=jax.ShapeDtypeStruct((8, 256), jnp.float32),
        in_specs=[
            vmem,
            pl.BlockSpec(memory_space=pl.ANY),
            pl.BlockSpec(memory_space=pltpu.SMEM),
            vmem,
        ],
        out_specs=vmem,
        scratch_shapes=[
            pltpu.VMEM((SHARDS, LOOPS, 16, D), jnp.bfloat16),
            pltpu.VMEM((ROWS, D_IN), jnp.bfloat16),
            pltpu.VMEM((ROWS, D), jnp.bfloat16),
            pltpu.VMEM((16, ROWS), jnp.bfloat16),
            pltpu.VMEM((2, 8, COLS), jnp.float32),
            pltpu.VMEM((ROWS, COLS), jnp.bfloat16),
            pltpu.VMEM((ROWS, COLS), jnp.bfloat16),
            dma,
            dma,
            dma((NZ,)),
            dma((NZ,)),
            dma((2, 5, 4)),
            dma((2, 5, 4)),
            dma((32,)),
            dma((32,)),
        ],
        compiler_params=pltpu.CompilerParams(
            collective_id=0, has_side_effects=True, vmem_limit_bytes=VMEM_LIMIT
        ),
        name="gather_maxsim",
    )(block, hidden, counts, w_proj)


def solution(mesh):
    in_specs = (
        P(("shard", "loop"), None),
        P(("shard", "loop")),
        P(("shard", "loop")),
        P(),
        P("loop", "shard", None),
    )
    out_specs = P(("shard", "loop"), None)
    return jax.shard_map(body, mesh=mesh, in_specs=in_specs, out_specs=out_specs, check_vma=False)
```

```python
import math

import jax
import jax.numpy as jnp
from jax import lax
from jax.experimental import pallas as pl
from jax.experimental.pallas import tpu as pltpu
from jax.sharding import PartitionSpec as P

BETA = 16.0
EPS = 1e-06
NX, NY, NZ = 4, 4, 16
ROWS, D_IN, D = 1920, 768, 128
SHARDS, LOOPS = 16, 32
MESH = pl.DeviceIdType.MESH
VMEM_LIMIT = 60 * 1024 * 1024


def unit_rows(values):
    values = values.astype(jnp.float32)
    return (values * lax.rsqrt(jnp.sum(values * values, axis=-1, keepdims=True) + EPS)).astype(
        jnp.bfloat16
    )


COLS = 512
CHUNKS = [(start, min(256, ROWS - start)) for start in range(0, ROWS, 256)]


def similarity(vectors, block, start, size):
    return lax.dot_general(
        vectors[pl.ds(start, size), :],
        block,
        (((1,), (1,)), ((), ())),
        preferred_element_type=jnp.float32,
    )


def overlapped(vectors, member, block, fill, drain):
    mass = jnp.zeros((16, COLS), jnp.float32)
    ahead = None
    if fill is not None:
        ahead = similarity(vectors, block, *CHUNKS[0])
    for position, (start, size) in enumerate(CHUNKS):
        now = ahead
        if fill is not None and position + 1 < len(CHUNKS):
            ahead = similarity(vectors, block, *CHUNKS[position + 1])
        if drain is not None:
            mass = mass + jnp.dot(
                member[:, pl.ds(start, size)],
                drain[pl.ds(start, size), :],
                preferred_element_type=jnp.float32,
            )
        if fill is not None:
            fill[pl.ds(start, size), :] = jnp.exp2(now * (BETA * math.log2(math.e))).astype(jnp.bfloat16)
    return mass[:8]


def prepare(hidden, counts, w_proj, vectors, member, totals):
    for start in range(0, ROWS, 384):
        projected = jnp.dot(
            hidden[pl.ds(start, 384), :], w_proj[...], preferred_element_type=jnp.float32
        )
        vectors[pl.ds(start, 384), :] = unit_rows(projected)
    docs = lax.broadcasted_iota(jnp.int32, (16, ROWS), 0)
    slots = lax.broadcasted_iota(jnp.int32, (16, ROWS), 1)
    rows = lax.broadcasted_iota(jnp.int32, (8, COLS), 0)
    inside = jnp.zeros((16, ROWS), jnp.bool_)
    lengths = jnp.ones((8, COLS), jnp.float32)
    first = jnp.int32(0)
    for doc in range(8):
        last = first + counts[doc]
        inside = inside | ((docs == doc) & (slots >= first) & (slots < last))
        lengths = jnp.where(rows == doc, counts[doc].astype(jnp.float32), lengths)
        first = last
    member[...] = jnp.where(inside, 1.0, 0.0).astype(jnp.bfloat16)
    totals[...] = jnp.zeros_like(totals)
    return lengths


def fused_kernel(
    seeds, hidden, counts, w_proj, out,
    own, buf, rows_in, vectors, member, totals, even, odd,
    local_sem, hidden_sem, send_z, recv_z, send_h, recv_h, send_c, recv_c,
):
    fetch = pltpu.make_async_copy(hidden, rows_in, hidden_sem)
    fetch.start()
    own[...] = unit_rows(seeds[...].astype(jnp.float32).reshape(16, D))
    me_s = lax.axis_index("shard")
    me_l = lax.axis_index("loop")
    core, y, x_lo = me_s % 2, (me_s // 2) % NY, me_s // (2 * NY)
    x_hi, z = me_l // NZ, me_l % NZ
    x = 2 * x_hi + x_lo

    def device(px, py, pz, pc):
        return (((px % 2) * NY + py) * 2 + pc, (px // 2) * NZ + pz)

    def moved(value, by, size):
        return (value + by + size) % size

    def place(half, a, b, c, low=0, count=8):
        dx, dy = (a, b) if half == 0 else (b, a)
        px, py = moved(x, dx, NX), moved(y, dy, NY)
        return buf.at[((px % 2) * NY + py) * 2 + c, pl.ds((px // 2) * NZ + 8 * half + low, count)]

    def neighbour(half, order, by):
        if (half == 0) == (order == 0):
            return device(moved(x, by, NX), y, z, core)
        return device(x, moved(y, by, NY), z, core)

    barrier = pltpu.get_barrier_semaphore()
    partners = [device(x, y, moved(z, k, NZ), core) for k in range(1, NZ)]
    partners += [neighbour(0, 0, 1), neighbour(0, 0, -1), neighbour(0, 1, 1), neighbour(0, 1, -1)]
    partners += [device(x, y, z, 1 - core)]
    for partner in partners:
        pl.semaphore_signal(barrier, inc=1, device_id=partner, device_id_type=MESH)
    pl.semaphore_wait(barrier, len(partners))

    sent = []

    def remote(src, dst, send, recv, target):
        return pltpu.make_async_remote_copy(
            src_ref=src, dst_ref=dst, send_sem=send, recv_sem=recv, device_id=target, device_id_type=MESH
        )

    def z_copy(k, block):
        return remote(own, block, send_z.at[k], recv_z.at[k], device(x, y, moved(z, k, NZ), core))

    def start(copy):
        copy.start()
        sent.append(copy)

    mine = pltpu.make_async_copy(own, buf.at[me_s, me_l], local_sem)
    mine.start()
    for k in (8, 7, 9, 6, 10, 5, 11, 4, 12, 3, 13, 2, 14, 1, 15):
        start(z_copy(k, buf.at[me_s, me_l]))
    fetch.wait()
    lengths = prepare(rows_in, counts, w_proj, vectors, member, totals)
    mine.wait()
    for k in range(1, NZ):
        z_copy(k, buf.at[me_s, x_hi * NZ + moved(z, -k, NZ)]).wait_recv()

    def hop(half, index, kind, ref, order):
        by = 1 if kind in (0, 2) else -1
        return remote(
            ref, ref, send_h.at[half, index, kind], recv_h.at[half, index, kind], neighbour(half, order, by)
        )

    def cross(half, a, b, c):
        ref = place(half, a, b, c)
        slot = (half * 4 + a % 4) * 4 + b % 4
        return remote(ref, ref, send_c.at[slot], recv_c.at[slot], device(x, y, z, 1 - core))

    def ready_first(half, a):
        start(hop(half, a % 4, 0, place(half, a, 0, core), 1))
        start(hop(half, a % 4, 1, place(half, a, 0, core), 1))
        start(cross(half, a, 0, core))

    halves = (0, 1)
    slabs = [(half, side) for half in halves for side in (-1, 1)]

    def first_arrived(half):
        hop(half, 4, 0, place(half, -1, 0, core), 0).wait_recv()
        start(hop(half, 4, 2, place(half, -1, 0, core, 0, 4), 0))
        hop(half, 4, 1, place(half, 1, 0, core), 0).wait_recv()
        start(hop(half, 4, 3, place(half, 1, 0, core, 4, 4), 0))
        ready_first(half, -1)
        ready_first(half, 1)

    def first_opposite(half):
        hop(half, 4, 2, place(half, 2, 0, core, 0, 4), 0).wait_recv()
        hop(half, 4, 3, place(half, 2, 0, core, 4, 4), 0).wait_recv()
        ready_first(half, 2)

    def second_arrived(half, a):
        hop(half, a % 4, 0, place(half, a, -1, core), 1).wait_recv()
        start(hop(half, a % 4, 2, place(half, a, -1, core, 0, 4), 1))
        hop(half, a % 4, 1, place(half, a, 1, core), 1).wait_recv()
        start(hop(half, a % 4, 3, place(half, a, 1, core, 4, 4), 1))
        start(cross(half, a, -1, core))
        start(cross(half, a, 1, core))

    def second_opposite(half, a):
        hop(half, a % 4, 2, place(half, a, 2, core, 0, 4), 1).wait_recv()
        hop(half, a % 4, 3, place(half, a, 2, core, 4, 4), 1).wait_recv()
        start(cross(half, a, 2, core))

    scratch = (even, odd)
    done = []

    def drained(block, fill, drain):
        mass = overlapped(vectors, member, block, fill, drain)
        if drain is not None:
            totals[done[-1]] += jnp.log(mass / lengths)

    def score(dx, dy):
        cross(0, dx, dy, 1 - core).wait_recv()
        cross(1, dy, dx, 1 - core).wait_recv()
        px, py = moved(x, dx, NX), moved(y, dy, NY)
        block = buf[pl.ds(((px % 2) * NY + py) * 2, 2), pl.ds((px // 2) * NZ, NZ)].reshape(COLS, D)
        turn = len(done)
        drained(block, scratch[turn % 2], scratch[(turn - 1) % 2] if turn else None)
        done.append(px // 2)

    for half in halves:
        own_slab = place(half, 0, 0, core)
        start(hop(half, 4, 0, own_slab, 0))
        start(hop(half, 4, 1, own_slab, 0))
    for half in halves:
        ready_first(half, 0)
    score(0, 0)
    for half in halves:
        first_arrived(half)
    for half in halves:
        second_arrived(half, 0)
    score(1, 0)
    for half in halves:
        first_opposite(half)
    score(-1, 0)
    for half, side in slabs:
        second_arrived(half, side)
    score(0, 1)
    score(0, -1)
    score(1, 1)
    for half in halves:
        second_arrived(half, 2)
    score(1, -1)
    for half in halves:
        second_opposite(half, 0)
    score(-1, 1)
    score(-1, -1)
    for half, side in slabs:
        second_opposite(half, side)
    for dx, dy in ((2, 0), (0, 2), (2, 1), (2, -1)):
        score(dx, dy)
    for half in halves:
        second_opposite(half, 2)
    for dx, dy in ((1, 2), (-1, 2), (2, 2)):
        score(dx, dy)
    drained(None, None, scratch[(len(done) - 1) % 2])
    pairs = (
        lax.broadcasted_iota(jnp.int32, (COLS // 2, COLS // 4), 0) // 2
        == lax.broadcasted_iota(jnp.int32, (COLS // 2, COLS // 4), 1)
    ).astype(jnp.float32)
    for side in range(2):
        both = totals[side][:, : COLS // 2] + totals[side][:, COLS // 2 :]
        out[:, pl.ds(side * (COLS // 4), COLS // 4)] = jnp.dot(
            both * (1.0 / 32.0),
            pairs,
            precision=lax.Precision.HIGHEST,
            preferred_element_type=jnp.float32,
        )
    for copy in sent:
        copy.wait_send()


def body(hidden, segment, counts, w_proj, seeds):
    vmem = pl.BlockSpec(memory_space=pltpu.VMEM)
    dma = pltpu.SemaphoreType.DMA
    return pl.pallas_call(
        fused_kernel,
        out_shape=jax.ShapeDtypeStruct((8, 256), jnp.float32),
        in_specs=[
            vmem,
            pl.BlockSpec(memory_space=pl.ANY),
            pl.BlockSpec(memory_space=pltpu.SMEM),
            vmem,
        ],
        out_specs=vmem,
        scratch_shapes=[
            pltpu.VMEM((16, D), jnp.bfloat16),
            pltpu.VMEM((SHARDS, LOOPS, 16, D), jnp.bfloat16),
            pltpu.VMEM((ROWS, D_IN), jnp.bfloat16),
            pltpu.VMEM((ROWS, D), jnp.bfloat16),
            pltpu.VMEM((16, ROWS), jnp.bfloat16),
            pltpu.VMEM((2, 8, COLS), jnp.float32),
            pltpu.VMEM((ROWS, COLS), jnp.bfloat16),
            pltpu.VMEM((ROWS, COLS), jnp.bfloat16),
            dma,
            dma,
            dma((NZ,)),
            dma((NZ,)),
            dma((2, 5, 4)),
            dma((2, 5, 4)),
            dma((32,)),
            dma((32,)),
        ],
        compiler_params=pltpu.CompilerParams(
            collective_id=0, has_side_effects=True, vmem_limit_bytes=VMEM_LIMIT
        ),
        name="gather_maxsim",
    )(seeds, hidden, counts, w_proj)


def solution(mesh):
    in_specs = (
        P(("shard", "loop"), None),
        P(("shard", "loop")),
        P(("shard", "loop")),
        P(),
        P("loop", "shard", None),
    )
    out_specs = P(("shard", "loop"), None)
    return jax.shard_map(body, mesh=mesh, in_specs=in_specs, out_specs=out_specs, check_vma=False)
```

```python
import math

import jax
import jax.numpy as jnp
from jax import lax
from jax.experimental import pallas as pl
from jax.experimental.pallas import tpu as pltpu
from jax.sharding import PartitionSpec as P

BETA = 16.0
EPS = 1e-06
NX, NY, NZ = 4, 4, 16
ROWS, D_IN, D = 1920, 768, 128
SHARDS, LOOPS = 16, 32
MESH = pl.DeviceIdType.MESH
VMEM_LIMIT = 60 * 1024 * 1024


def unit_rows(values):
    values = values.astype(jnp.float32)
    return (values * lax.rsqrt(jnp.sum(values * values, axis=-1, keepdims=True) + EPS)).astype(
        jnp.bfloat16
    )


COLS = 512
CHUNKS = [(start, min(512, ROWS - start)) for start in range(0, ROWS, 512)]


def similarity(vectors, block, start, size):
    return lax.dot_general(
        vectors[pl.ds(start, size), :],
        block,
        (((1,), (1,)), ((), ())),
        preferred_element_type=jnp.float32,
    )


def overlapped(vectors, member, block, fill, drain):
    mass = jnp.zeros((16, COLS), jnp.float32)
    ahead = None
    if fill is not None:
        ahead = similarity(vectors, block, *CHUNKS[0])
    for position, (start, size) in enumerate(CHUNKS):
        now = ahead
        if fill is not None and position + 1 < len(CHUNKS):
            ahead = similarity(vectors, block, *CHUNKS[position + 1])
        if drain is not None:
            mass = mass + jnp.dot(
                member[:, pl.ds(start, size)],
                drain[pl.ds(start, size), :],
                preferred_element_type=jnp.float32,
            )
        if fill is not None:
            fill[pl.ds(start, size), :] = jnp.exp2(now * (BETA * math.log2(math.e))).astype(jnp.bfloat16)
    return mass[:8]


def prepare(hidden, counts, w_proj, vectors, member, totals):
    for start in range(0, ROWS, 384):
        projected = jnp.dot(
            hidden[pl.ds(start, 384), :], w_proj[...], preferred_element_type=jnp.float32
        )
        vectors[pl.ds(start, 384), :] = unit_rows(projected)
    docs = lax.broadcasted_iota(jnp.int32, (16, ROWS), 0)
    slots = lax.broadcasted_iota(jnp.int32, (16, ROWS), 1)
    rows = lax.broadcasted_iota(jnp.int32, (8, COLS), 0)
    inside = jnp.zeros((16, ROWS), jnp.bool_)
    lengths = jnp.ones((8, COLS), jnp.float32)
    first = jnp.int32(0)
    for doc in range(8):
        last = first + counts[doc]
        inside = inside | ((docs == doc) & (slots >= first) & (slots < last))
        lengths = jnp.where(rows == doc, counts[doc].astype(jnp.float32), lengths)
        first = last
    member[...] = jnp.where(inside, 1.0, 0.0).astype(jnp.bfloat16)
    totals[...] = jnp.zeros_like(totals)
    return lengths


def fused_kernel(
    seeds, hidden, counts, w_proj, out,
    own, buf, rows_in, vectors, member, totals, even, odd,
    local_sem, hidden_sem, send_z, recv_z, send_h, recv_h, send_c, recv_c,
):
    fetch = pltpu.make_async_copy(hidden, rows_in, hidden_sem)
    fetch.start()
    own[...] = unit_rows(seeds[...].astype(jnp.float32).reshape(16, D))
    me_s = lax.axis_index("shard")
    me_l = lax.axis_index("loop")
    core, y, x_lo = me_s % 2, (me_s // 2) % NY, me_s // (2 * NY)
    x_hi, z = me_l // NZ, me_l % NZ
    x = 2 * x_hi + x_lo

    def device(px, py, pz, pc):
        return (((px % 2) * NY + py) * 2 + pc, (px // 2) * NZ + pz)

    def moved(value, by, size):
        return (value + by + size) % size

    def place(half, a, b, c, low=0, count=8):
        dx, dy = (a, b) if half == 0 else (b, a)
        px, py = moved(x, dx, NX), moved(y, dy, NY)
        return buf.at[((px % 2) * NY + py) * 2 + c, pl.ds((px // 2) * NZ + 8 * half + low, count)]

    def neighbour(half, order, by):
        if (half == 0) == (order == 0):
            return device(moved(x, by, NX), y, z, core)
        return device(x, moved(y, by, NY), z, core)

    barrier = pltpu.get_barrier_semaphore()
    partners = [device(x, y, moved(z, k, NZ), core) for k in range(1, NZ)]
    partners += [neighbour(0, 0, 1), neighbour(0, 0, -1), neighbour(0, 1, 1), neighbour(0, 1, -1)]
    partners += [device(x, y, z, 1 - core)]
    for partner in partners:
        pl.semaphore_signal(barrier, inc=1, device_id=partner, device_id_type=MESH)
    pl.semaphore_wait(barrier, len(partners))

    sent = []

    def remote(src, dst, send, recv, target):
        return pltpu.make_async_remote_copy(
            src_ref=src, dst_ref=dst, send_sem=send, recv_sem=recv, device_id=target, device_id_type=MESH
        )

    def z_copy(k, block):
        return remote(own, block, send_z.at[k], recv_z.at[k], device(x, y, moved(z, k, NZ), core))

    def start(copy):
        copy.start()
        sent.append(copy)

    mine = pltpu.make_async_copy(own, buf.at[me_s, me_l], local_sem)
    mine.start()
    for k in (8, 7, 9, 6, 10, 5, 11, 4, 12, 3, 13, 2, 14, 1, 15):
        start(z_copy(k, buf.at[me_s, me_l]))
    fetch.wait()
    lengths = prepare(rows_in, counts, w_proj, vectors, member, totals)
    mine.wait()
    for k in range(1, NZ):
        z_copy(k, buf.at[me_s, x_hi * NZ + moved(z, -k, NZ)]).wait_recv()

    def hop(half, index, kind, ref, order):
        by = 1 if kind in (0, 2) else -1
        return remote(
            ref, ref, send_h.at[half, index, kind], recv_h.at[half, index, kind], neighbour(half, order, by)
        )

    def cross(half, a, b, c):
        ref = place(half, a, b, c)
        slot = (half * 4 + a % 4) * 4 + b % 4
        return remote(ref, ref, send_c.at[slot], recv_c.at[slot], device(x, y, z, 1 - core))

    def ready_first(half, a):
        start(hop(half, a % 4, 0, place(half, a, 0, core), 1))
        start(hop(half, a % 4, 1, place(half, a, 0, core), 1))
        start(cross(half, a, 0, core))

    halves = (0, 1)
    slabs = [(half, side) for half in halves for side in (-1, 1)]

    def first_arrived(half):
        hop(half, 4, 0, place(half, -1, 0, core), 0).wait_recv()
        start(hop(half, 4, 2, place(half, -1, 0, core, 0, 4), 0))
        hop(half, 4, 1, place(half, 1, 0, core), 0).wait_recv()
        start(hop(half, 4, 3, place(half, 1, 0, core, 4, 4), 0))
        ready_first(half, -1)
        ready_first(half, 1)

    def first_opposite(half):
        hop(half, 4, 2, place(half, 2, 0, core, 0, 4), 0).wait_recv()
        hop(half, 4, 3, place(half, 2, 0, core, 4, 4), 0).wait_recv()
        ready_first(half, 2)

    def second_arrived(half, a):
        hop(half, a % 4, 0, place(half, a, -1, core), 1).wait_recv()
        start(hop(half, a % 4, 2, place(half, a, -1, core, 0, 4), 1))
        hop(half, a % 4, 1, place(half, a, 1, core), 1).wait_recv()
        start(hop(half, a % 4, 3, place(half, a, 1, core, 4, 4), 1))
        start(cross(half, a, -1, core))
        start(cross(half, a, 1, core))

    def second_opposite(half, a):
        hop(half, a % 4, 2, place(half, a, 2, core, 0, 4), 1).wait_recv()
        hop(half, a % 4, 3, place(half, a, 2, core, 4, 4), 1).wait_recv()
        start(cross(half, a, 2, core))

    scratch = (even, odd)
    done = []

    def drained(block, fill, drain):
        mass = overlapped(vectors, member, block, fill, drain)
        if drain is not None:
            totals[done[-1]] += jnp.log(mass / lengths)

    def score(dx, dy):
        cross(0, dx, dy, 1 - core).wait_recv()
        cross(1, dy, dx, 1 - core).wait_recv()
        px, py = moved(x, dx, NX), moved(y, dy, NY)
        block = buf[pl.ds(((px % 2) * NY + py) * 2, 2), pl.ds((px // 2) * NZ, NZ)].reshape(COLS, D)
        turn = len(done)
        drained(block, scratch[turn % 2], scratch[(turn - 1) % 2] if turn else None)
        done.append(px // 2)

    for half in halves:
        own_slab = place(half, 0, 0, core)
        start(hop(half, 4, 0, own_slab, 0))
        start(hop(half, 4, 1, own_slab, 0))
    for half in halves:
        ready_first(half, 0)
    score(0, 0)
    for half in halves:
        first_arrived(half)
    for half in halves:
        second_arrived(half, 0)
    score(1, 0)
    for half in halves:
        first_opposite(half)
    score(-1, 0)
    for half, side in slabs:
        second_arrived(half, side)
    score(0, 1)
    score(0, -1)
    score(1, 1)
    for half in halves:
        second_arrived(half, 2)
    score(1, -1)
    for half in halves:
        second_opposite(half, 0)
    score(-1, 1)
    score(-1, -1)
    for half, side in slabs:
        second_opposite(half, side)
    for dx, dy in ((2, 0), (0, 2), (2, 1), (2, -1)):
        score(dx, dy)
    for half in halves:
        second_opposite(half, 2)
    for dx, dy in ((1, 2), (-1, 2), (2, 2)):
        score(dx, dy)
    drained(None, None, scratch[(len(done) - 1) % 2])
    pairs = (
        lax.broadcasted_iota(jnp.int32, (COLS // 2, COLS // 4), 0) // 2
        == lax.broadcasted_iota(jnp.int32, (COLS // 2, COLS // 4), 1)
    ).astype(jnp.float32)
    for side in range(2):
        both = totals[side][:, : COLS // 2] + totals[side][:, COLS // 2 :]
        out[:, pl.ds(side * (COLS // 4), COLS // 4)] = jnp.dot(
            both * (1.0 / 32.0),
            pairs,
            precision=lax.Precision.HIGHEST,
            preferred_element_type=jnp.float32,
        )
    for copy in sent:
        copy.wait_send()


def body(hidden, segment, counts, w_proj, seeds):
    vmem = pl.BlockSpec(memory_space=pltpu.VMEM)
    dma = pltpu.SemaphoreType.DMA
    return pl.pallas_call(
        fused_kernel,
        out_shape=jax.ShapeDtypeStruct((8, 256), jnp.float32),
        in_specs=[
            vmem,
            pl.BlockSpec(memory_space=pl.ANY),
            pl.BlockSpec(memory_space=pltpu.SMEM),
            vmem,
        ],
        out_specs=vmem,
        scratch_shapes=[
            pltpu.VMEM((16, D), jnp.bfloat16),
            pltpu.VMEM((SHARDS, LOOPS, 16, D), jnp.bfloat16),
            pltpu.VMEM((ROWS, D_IN), jnp.bfloat16),
            pltpu.VMEM((ROWS, D), jnp.bfloat16),
            pltpu.VMEM((16, ROWS), jnp.bfloat16),
            pltpu.VMEM((2, 8, COLS), jnp.float32),
            pltpu.VMEM((ROWS, COLS), jnp.bfloat16),
            pltpu.VMEM((ROWS, COLS), jnp.bfloat16),
            dma,
            dma,
            dma((NZ,)),
            dma((NZ,)),
            dma((2, 5, 4)),
            dma((2, 5, 4)),
            dma((32,)),
            dma((32,)),
        ],
        compiler_params=pltpu.CompilerParams(
            collective_id=0, has_side_effects=True, vmem_limit_bytes=VMEM_LIMIT
        ),
        name="gather_maxsim",
    )(seeds, hidden, counts, w_proj)


def solution(mesh):
    in_specs = (
        P(("shard", "loop"), None),
        P(("shard", "loop")),
        P(("shard", "loop")),
        P(),
        P("loop", "shard", None),
    )
    out_specs = P(("shard", "loop"), None)
    return jax.shard_map(body, mesh=mesh, in_specs=in_specs, out_specs=out_specs, check_vma=False)
```
